32 devices in a mesh: dp: 2 (over core), seq: 16 (over z, y, x).
Axes of the slice: x: 2, y: 2, z: 4, core: 2. Of those that a mesh axis runs over, the one named last changes fastest.
Arguments:
- queries: bfloat16 [2, 4096, 2048], P('dp', 'seq'), may hold values from -6 to 6
- keys: bfloat16 [2, 4096, 2048], P('dp', 'seq'), may hold values from -6 to 6
- values: bfloat16 [2, 4096, 2048], P('dp', 'seq'), may hold values from -6 to 6
- out_grad: bfloat16 [2, 4096, 4096], P('dp', 'seq'), may hold values from -6 to 6
- out_weight: bfloat16 [2048, 4096], replicated, may hold values from -0.125 to 0.125
Outputs:
- attended: bfloat16 [2, 4096, 2048], P('dp', 'seq')
- query_grad: bfloat16 [2, 4096, 2048], P('dp', 'seq')
- key_grad: bfloat16 [2, 4096, 2048], P('dp', 'seq')
- value_grad: bfloat16 [2, 4096, 2048], P('dp', 'seq')
- weight_grad: float32 [2048, 4096], P(('dp', 'seq'))
The draws below stay inside these ranges and needn't reach their ends.
All inputs are finite; a program needn't handle non-finite values.
Results may differ from the reference program's by a relative error of at most 0.0051.
Values sent between devices are 32-bit elements; how exact they have to be, the bound alone decides.
No kernel may reach another device: no remote copies, remote signals or barrier semaphores. Data moves between devices by JAX's collectives and lax.ppermute only.
A program may use at most 192 MiB of HBM per device.

```python
import jax
import jax.numpy as jnp
from jax import lax

D = 4096
P_SIZE = 128
H = 16
TOK_DEV = 256
HD = 2048
LEN = 4096
SEQS = 2
N_SEQ = 16


def level_of(own_key, dims, pieces, smallest, high):
    def one(dim, parts):
        draws = jax.random.uniform(jax.random.fold_in(jax.random.fold_in(own_key, 6), dim), (parts,), jnp.float32, smallest / len(pieces), high / len(pieces))
        return jnp.repeat(jnp.exp(draws), dims[dim] // parts).reshape((-1,) + (1,) * (len(dims) - dim - 1))

    gain = one(*pieces[0])
    for cut in pieces[1:]:
        gain = gain * one(*cut)
    return gain


def noise(own_key, extent, width, bound, split=(), kind=jnp.bfloat16):
    values = width * jax.random.normal(own_key, extent, jnp.float32)
    if split:
        values = values * level_of(own_key, extent, split, -0.22, 0.18)
    return jnp.clip(values, -bound, bound).astype(kind)


def setup_inputs(seed: int = 0) -> dict:
    seeds = jax.random.split(jax.random.key(seed), 6)
    return {
        "queries": noise(seeds[0], (SEQS, LEN, HD), 1.0, 6.0, ((0, 2), (1, 16))),
        "keys": noise(seeds[1], (SEQS, LEN, HD), 1.0, 6.0, ((0, 2), (1, 16))),
        "values": noise(seeds[2], (SEQS, LEN, HD), 1.0, 6.0, ((0, 2), (1, 16))),
        "out_grad": noise(seeds[3], (SEQS, LEN, D), 1.0, 6.0, ((0, 2), (1, 16))),
        "out_weight": noise(seeds[4], (HD, D), HD ** -0.5, 0.125),
    }


EPS = 1e-06
HIGH = lax.Precision.HIGHEST

def span_forward(qf, kf, vf, prefix):
    count = qf.shape[0]
    scores = jnp.einsum('thp,shp->hts', qf, kf, precision=HIGH)
    lower = jnp.arange(count)[:, None] >= jnp.arange(count)[None, :]
    probs = jnp.where(lower[None], scores, 0.0).astype(jnp.bfloat16)
    intra = jnp.einsum('hts,shp->thp', probs.astype(jnp.float32), vf, precision=HIGH)
    inter = jnp.einsum('thp,hpe->the', qf, prefix, precision=HIGH)
    outputs = intra + inter
    inverse = lax.rsqrt(lax.optimization_barrier(jnp.mean(outputs * outputs, axis=-1, keepdims=True)) + EPS)
    return (outputs, inverse, probs)

def span_backward(qf, kf, vf, prefix, probs, d_out):
    count = qf.shape[0]
    dof = d_out.astype(jnp.float32)
    lower = jnp.arange(count)[:, None] >= jnp.arange(count)[None, :]
    d_scores = jnp.einsum('the,she->hts', dof, vf, precision=HIGH)
    d_probs = jnp.where(lower[None], d_scores, 0.0).astype(jnp.bfloat16).astype(jnp.float32)
    d_query = jnp.einsum('hts,shp->thp', d_probs, kf, precision=HIGH) + jnp.einsum('the,hpe->thp', dof, prefix, precision=HIGH)
    d_key = jnp.einsum('hts,thp->shp', d_probs, qf, precision=HIGH)
    d_value = jnp.einsum('hts,the->she', probs.astype(jnp.float32), dof, precision=HIGH)
    d_prefix = jnp.einsum('thp,the->hpe', qf, dof, precision=HIGH)
    return (d_query, d_key, d_value, d_prefix)

def one_sequence(queries, keys, values, out_grad, out_weight):
    shape = (N_SEQ, TOK_DEV, H, P_SIZE)
    qf = queries.reshape(shape).astype(jnp.float32)
    kf = keys.reshape(shape).astype(jnp.float32)
    vf = values.reshape(shape).astype(jnp.float32)
    states = jnp.einsum('cshp,cshe->chpe', kf, vf, precision=HIGH)
    running = jnp.cumsum(states, axis=0)
    prefix = jnp.concatenate([jnp.zeros_like(states[:1]), running[:-1]], axis=0)
    outputs, inverse, probs = jax.vmap(span_forward)(qf, kf, vf, prefix)
    normed = outputs * inverse
    attended = normed.astype(jnp.bfloat16)
    grad = jnp.dot(out_grad.astype(jnp.float32), out_weight.astype(jnp.float32).T, precision=HIGH).reshape(shape)
    d_out = (inverse * (grad - normed * lax.optimization_barrier(jnp.mean(grad * normed, axis=-1, keepdims=True)))).astype(jnp.bfloat16)
    d_query, d_key, d_value, d_prefix = jax.vmap(span_backward)(qf, kf, vf, prefix, probs, d_out)
    later = jnp.cumsum(d_prefix[::-1], axis=0)[::-1]
    suffix = jnp.concatenate([later[1:], jnp.zeros_like(later[:1])], axis=0)
    d_key = d_key + jnp.einsum('cshe,chpe->cshp', vf, suffix, precision=HIGH)
    d_value = d_value + jnp.einsum('cshp,chpe->cshe', kf, suffix, precision=HIGH)
    flat = (LEN, HD)
    return (attended.reshape(flat), d_query.astype(jnp.bfloat16).reshape(flat), d_key.astype(jnp.bfloat16).reshape(flat), d_value.astype(jnp.bfloat16).reshape(flat))

def reference(queries, keys, values, out_grad, out_weight):

    def apply(items):
        return one_sequence(items[0], items[1], items[2], items[3], out_weight)
    attended, query_grad, key_grad, value_grad = lax.map(apply, (queries, keys, values, out_grad))
    every = attended.reshape(SEQS * LEN, HD).astype(jnp.float32)
    cotangent = out_grad.reshape(SEQS * LEN, D).astype(jnp.float32)
    weight_grad = jnp.dot(every.T, cotangent, precision=HIGH)
    return (attended, query_grad, key_grad, value_grad, weight_grad)
```

```python
import functools
import itertools

import jax
import jax.numpy as jnp
from jax import lax
from jax.experimental import pallas as pl
from jax.experimental.pallas import tpu as pltpu
from jax.sharding import PartitionSpec as P

P_SIZE = 128
EPS = 1e-06
AXES = ("dp", "seq")
CHUNKS = 2
F32 = jnp.float32
BF16 = jnp.bfloat16


VMEM = pl.BlockSpec(memory_space=pltpu.VMEM)
SMEM = pl.BlockSpec(memory_space=pltpu.SMEM)


def grid_of(count):
    power = count.bit_length() - 1
    if 1 << power != count:
        return count, 1, 1
    z = -(-power // 3)
    y = -(-(power - z) // 2)
    return 1 << z, 1 << y, 1 << (power - z - y)


def tn(a, b):
    return lax.dot_general(a, b, (((0,), (0,)), ((), ())), preferred_element_type=F32)


def nt(a, b):
    return lax.dot_general(a, b, (((1,), (1,)), ((), ())), preferred_element_type=F32)


def nn(a, b):
    return lax.dot_general(a, b, (((1,), (0,)), ((), ())), preferred_element_type=F32)


def halves(x):
    high = x.astype(BF16)
    return high, (x - high.astype(F32)).astype(BF16)


def head_at(part, heads, i):
    return pl.ds(pl.multiple_of((part * heads + i) * P_SIZE, P_SIZE), P_SIZE)


def lower_of(count):
    rows = lax.broadcasted_iota(jnp.int32, (count, count), 0)
    return rows >= lax.broadcasted_iota(jnp.int32, (count, count), 1)


def state_kernel(parts, index, k, v, *outs):
    heads = outs[0].shape[0]
    for o in range(parts):

        def one(i, carry, o=o):
            at = head_at(index[o], heads, i)
            outs[o][i] = tn(k[:, at], v[:, at])
            return carry

        lax.fori_loop(0, heads, one, 0)


def intra_kernel(q, k, v, probs, intra):
    scores = nt(q[...], k[...])
    kept = jnp.where(lower_of(scores.shape[0]), scores, 0.0).astype(BF16)
    probs[0] = kept
    intra[...] = nn(kept, v[...])


def output_kernel(parts, order, index, q, intra, grad, *refs):
    prefix, (attended, flipped, d_out), d_prefix = refs[:parts], refs[parts : parts + 3], refs[parts + 3 :]
    heads = prefix[0].shape[0]
    for o in range(parts):

        def one(i, carry, o=o):
            at = head_at(index[o], heads, i)
            query = q[:, at]
            high, low = halves(prefix[o][i])
            out = intra[:, at] + (nn(query, high) + nn(query, low))
            inverse = lax.rsqrt(jnp.mean(out * out, axis=-1, keepdims=True) + EPS)
            normed = out * inverse
            rounded = normed.astype(BF16)
            attended[:, at] = rounded
            flipped[at, :] = rounded.astype(F32).T
            cot = grad[:, at]
            mean = jnp.mean(cot * normed, axis=-1, keepdims=True)
            d = (inverse * (cot - normed * mean)).astype(BF16)
            d_out[:, at] = d
            d_prefix[order[o]][i] = tn(query, d)
            return carry

        lax.fori_loop(0, heads, one, 0)


def query_kernel(parts, index, k, v, d_out, *refs):
    prefix, (query_grad,) = refs[:parts], refs[parts:]
    heads = prefix[0].shape[0]
    lower = lower_of(k.shape[0])
    for o in range(parts):

        def one(i, carry, o=o):
            at = head_at(index[o], heads, i)
            d = d_out[:, at]
            high, low = halves(prefix[o][i])
            d_probs = jnp.where(lower, nt(d, v[:, at]), 0.0).astype(BF16)
            total = nn(d_probs, k[:, at]) + (nt(d, high) + nt(d, low))
            query_grad[:, at] = total.astype(BF16)
            return carry

        lax.fori_loop(0, heads, one, 0)


def key_value_kernel(parts, index, q, k, v, d_out, probs, *refs):
    suffix, (key_grad, value_grad) = refs[:parts], refs[parts:]
    heads = suffix[0].shape[0]
    lower = lower_of(k.shape[0])
    for o in range(parts):

        def one(i, carry, o=o):
            at = head_at(index[o], heads, i)
            d, value, key = d_out[:, at], v[:, at], k[:, at]
            high, low = halves(suffix[o][i])
            d_probs = jnp.where(lower, nt(d, value), 0.0).astype(BF16)
            d_key = tn(d_probs, q[:, at]) + (nt(value, high) + nt(value, low))
            key_grad[:, at] = d_key.astype(BF16)
            d_value = tn(probs[index[o] * heads + i], d) + (nn(key, high) + nn(key, low))
            value_grad[:, at] = d_value.astype(BF16)
            return carry

        lax.fori_loop(0, heads, one, 0)


def call(kernel, name, outs, flops, *args):
    moved = sum(a.size * a.dtype.itemsize for a in list(args) + list(outs))
    return pl.pallas_call(
        kernel,
        name=name,
        out_shape=tuple(outs),
        in_specs=[SMEM] + [VMEM] * (len(args) - 1),
        out_specs=(VMEM,) * len(outs),
        cost_estimate=pl.CostEstimate(flops=flops, bytes_accessed=moved, transcendentals=0),
        compiler_params=pltpu.CompilerParams(vmem_limit_bytes=40 << 20),
    )(*args)


def narrow_kernel(axis, *refs):
    out, at = refs[-1], 0
    for ref in refs[:-1]:
        size = ref.shape[axis]
        span = (pl.ds(at, size), slice(None)) if axis == 0 else (slice(None), pl.ds(at, size))
        out[span] = ref[...].astype(BF16)
        at += size


def narrow(pieces, axis):
    shape = list(pieces[0].shape)
    shape[axis] = sum(piece.shape[axis] for piece in pieces)
    moved = sum(6 * piece.size for piece in pieces)
    return pl.pallas_call(
        functools.partial(narrow_kernel, axis),
        name="narrow",
        out_shape=jax.ShapeDtypeStruct(tuple(shape), BF16),
        in_specs=[VMEM] * len(pieces),
        out_specs=VMEM,
        cost_estimate=pl.CostEstimate(flops=0, bytes_accessed=moved, transcendentals=0),
    )(*pieces)


def body(cores, count, queries, keys, values, out_grad, out_weight):
    dz, dy, dx = grid_of(count)
    plane = dy * dx
    tokens, width = queries.shape[1:]
    columns = out_grad.shape[-1]
    total_heads = width // P_SIZE
    heads = total_heads // plane
    block = width // (cores * count)
    q, k, v, cot = queries[0], keys[0], values[0], out_grad[0]

    core = lax.axis_index("dp")
    place = lax.axis_index("seq")
    x, y, z = place % dx, place // dx % dy, place // plane
    here = y * dx + x

    def send(value, to):
        pairs = []
        for d, a, b, c in itertools.product(range(cores), range(dz), range(dy), range(dx)):
            t = to(d, a, b, c)
            if t is not None:
                pairs.append((d * count + (a * dy + b) * dx + c, t[0] * count + (t[1] * dy + t[2]) * dx + t[3]))
        return lax.ppermute(value, AXES, pairs)

    def by(d=0, b=0, c=0):
        return lambda i, j, l, n: ((i + d) % cores, j, (l + b) % dy, (n + c) % dx)

    def along(step):
        return lambda i, j, l, n: (i, j + step, l, n) if 0 <= j + step < dz else None

    offsets = [(b, c) for b in range(dy) for c in range(dx)]
    target = [(y + b) % dy * dx + (x + c) % dx for b, c in offsets]
    source = [(y - b) % dy * dx + (x - c) % dx for b, c in offsets]
    order = [(-b % dy) * dx + (-c % dx) for b, c in offsets]
    target_index = jnp.stack(target).astype(jnp.int32)
    source_index = jnp.stack(source).astype(jnp.int32)

    part_shape = jax.ShapeDtypeStruct((heads, P_SIZE, P_SIZE), F32)
    wide = lambda kind: jax.ShapeDtypeStruct((tokens, width), kind)
    unit = 2 * tokens * width * P_SIZE

    def gather_plane(parts):
        return [parts[0]] + [send(parts[o], by(0, *offsets[o])) for o in range(1, plane)]

    def carry(received, sign):
        total = functools.reduce(jnp.add, received)
        carried, running, step = jnp.zeros_like(total), total, 1
        while step < dz:
            arrived = send(running, along(sign * step))
            carried, running, step = carried + arrived, running + arrived, 2 * step
        outs = []
        for o in range(plane):
            value = carried
            for s in range(plane):
                ahead = source[s] < target[o] if sign > 0 else source[s] > target[o]
                value = value + jnp.where(ahead, received[s], 0.0)
            outs.append(value)
        return total, outs

    states = call(functools.partial(state_kernel, plane), "states", [part_shape] * plane, unit, target_index, k, v)
    received = gather_plane(states)

    half = columns // 2
    size = half // CHUNKS
    wide_cot = cot.astype(F32)
    pieces = [[wide_cot[:, g * half + n * size : g * half + (n + 1) * size] for n in range(CHUNKS)] for g in (0, 1)]
    reach = (dx, dy)
    shift = (lambda d, o: by(d, 0, o), lambda d, o: by(d, o, 0))

    def spread(group, n):
        own = pieces[group][n]
        near = [own] + [send(own, shift[group](0, o)) for o in range(1, reach[group])]
        rows = list(near)
        for d in range(1, cores):
            rows += [send(value, by(d)) for value in near]
        return narrow(rows, 0)

    prefix_total, prefix_out = carry(received, 1)
    for n in range(CHUNKS):
        if n == 0:
            gate = prefix_total
            pieces[0][n], pieces[1][n], _ = lax.optimization_barrier((pieces[0][n], pieces[1][n], gate))
    prefix = gather_plane(prefix_out)
    for n in range(1, CHUNKS):
        pieces[0][n], pieces[1][n], _ = lax.optimization_barrier((pieces[0][n], pieces[1][n], prefix[-1]))
    spreads = [[spread(group, n) for n in range(CHUNKS)] for group in (0, 1)]

    head_block = pl.BlockSpec((tokens, P_SIZE), lambda h: (0, h))
    probs, intra = pl.pallas_call(
        intra_kernel,
        name="intra",
        grid=(total_heads,),
        out_shape=(jax.ShapeDtypeStruct((total_heads, tokens, tokens), BF16), wide(F32)),
        in_specs=[head_block] * 3,
        out_specs=(pl.BlockSpec((1, tokens, tokens), lambda h: (h, 0, 0)), head_block),
        cost_estimate=pl.CostEstimate(flops=4 * unit, bytes_accessed=14 * tokens * width, transcendentals=0),
    )(q, k, v)
    grad = nt(cot, out_weight)

    done = call(
        functools.partial(output_kernel, plane, order),
        "outputs",
        [wide(BF16), jax.ShapeDtypeStruct((width, tokens), F32), wide(BF16)] + [part_shape] * plane,
        4 * unit,
        source_index, q, intra, grad, *prefix,
    )
    attended, flipped, d_out, d_prefix = done[0], done[1], done[2], done[3:]

    d_received = gather_plane(d_prefix)

    folded = flipped.reshape(cores, dz, dy, dx, block, tokens)

    def features(group):
        mine, axis = ((x, 3), (y, 2))[group]
        near = reach[group]
        sides = []
        for d in range(cores):
            for o in range(near):
                pick = lax.dynamic_index_in_dim(folded, (core + d) % cores, 0, False)
                pick = lax.dynamic_index_in_dim(pick, (mine + o) % near, axis - 1, False)
                sides.append(pick if d == 0 and o == 0 else send(pick, shift[group](d, o)))
        return narrow([side.reshape(-1, tokens) for side in sides], 1)

    _, suffix_out = carry(d_received, -1)
    suffix = gather_plane(suffix_out)

    left = [features(0), features(1)]

    def first_stage(group, n):
        near = (dy, dx)[group]
        mine = (y, x)[group]
        other = (lambda o: by(0, o, 0), lambda o: by(0, 0, o))[group]
        right = spreads[group][n]

        def partial(o):
            rows = lax.dynamic_index_in_dim(left[group].reshape(dz, near, block, -1), (mine + o) % near, 1, False)
            return nn(rows.reshape(dz * block, -1), right).reshape(dz, block, size)

        arrived = [send(partial(o), other(o)) for o in range(1, near)]
        return functools.reduce(jnp.add, [partial(0)] + arrived)

    def line(sums):
        up = down = None
        for d in range(dz - 1, 0, -1):
            above = lax.dynamic_index_in_dim(sums, (z + d) % dz, 0, False)
            below = lax.dynamic_index_in_dim(sums, (z - d) % dz, 0, False)
            above = above if up is None else above + up
            below = below if down is None else below + down
            up = send(above, lambda i, j, l, n: (i, j + 1, l, n) if j + d < dz else None)
            down = send(below, lambda i, j, l, n: (i, j - 1, l, n) if j - d >= 0 else None)
        own = lax.dynamic_index_in_dim(sums, z, 0, False)
        return own if up is None else own + up + down

    chunks = []
    for n in range(CHUNKS):
        sums = jnp.concatenate([first_stage(0, n), first_stage(1, n)], axis=-1)
        chunks.append(line(sums))
    weight_grad = jnp.concatenate([c[:, :size] for c in chunks] + [c[:, size:] for c in chunks], axis=-1)

    (query_grad,) = call(
        functools.partial(query_kernel, plane), "query", [wide(BF16)], 6 * unit, source_index, k, v, d_out, *prefix
    )
    key_grad, value_grad = call(
        functools.partial(key_value_kernel, plane),
        "keys",
        [wide(BF16), wide(BF16)],
        10 * unit,
        source_index, q, k, v, d_out, probs, *suffix,
    )
    return attended[None], query_grad[None], key_grad[None], value_grad[None], weight_grad


def solution(mesh):
    spec = P("dp", "seq", None)
    return jax.shard_map(
        functools.partial(body, mesh.shape["dp"], mesh.shape["seq"]),
        mesh=mesh,
        in_specs=(spec,) * 4 + (P(),),
        out_specs=(spec,) * 4 + (P(AXES, None),),
        check_vma=False,
    )
```

```python
import functools
import itertools

import jax
import jax.numpy as jnp
from jax import lax
from jax.experimental import pallas as pl
from jax.experimental.pallas import tpu as pltpu
from jax.sharding import PartitionSpec as P

P_SIZE = 128
EPS = 1e-06
AXES = ("dp", "seq")
CHUNKS = 2
EARLY = 8
F32 = jnp.float32
BF16 = jnp.bfloat16


VMEM = pl.BlockSpec(memory_space=pltpu.VMEM)
SMEM = pl.BlockSpec(memory_space=pltpu.SMEM)


def grid_of(count):
    power = count.bit_length() - 1
    if 1 << power != count:
        return count, 1, 1
    z = -(-power // 3)
    y = -(-(power - z) // 2)
    return 1 << z, 1 << y, 1 << (power - z - y)


def tn(a, b):
    return lax.dot_general(a, b, (((0,), (0,)), ((), ())), preferred_element_type=F32)


def nt(a, b):
    return lax.dot_general(a, b, (((1,), (1,)), ((), ())), preferred_element_type=F32)


def nn(a, b):
    return lax.dot_general(a, b, (((1,), (0,)), ((), ())), preferred_element_type=F32)


def halves(x):
    high = x.astype(BF16)
    return high, (x - high.astype(F32)).astype(BF16)


def head_at(part, heads, i):
    return pl.ds(pl.multiple_of((part * heads + i) * P_SIZE, P_SIZE), P_SIZE)


def lower_of(count):
    rows = lax.broadcasted_iota(jnp.int32, (count, count), 0)
    return rows >= lax.broadcasted_iota(jnp.int32, (count, count), 1)


def state_kernel(parts, index, k, v, *outs):
    heads = outs[0].shape[0]
    for o in range(parts):

        def one(i, carry, o=o):
            at = head_at(index[o], heads, i)
            outs[o][i] = tn(k[:, at], v[:, at])
            return carry

        lax.fori_loop(0, heads, one, 0)


def intra_kernel(q, k, v, probs, intra):
    scores = nt(q[...], k[...])
    kept = jnp.where(lower_of(scores.shape[0]), scores, 0.0).astype(BF16)
    probs[0] = kept
    intra[...] = nn(kept, v[...])


def output_kernel(parts, order, index, q, intra, low_grad, high_grad, *refs):
    prefix, (attended, flipped, d_out), d_prefix = refs[:parts], refs[parts : parts + 3], refs[parts + 3 :]
    heads = prefix[0].shape[0]
    for o in range(parts):

        def one(i, carry, o=o):
            at = head_at(index[o], heads, i)
            query = q[:, at]
            high, low = halves(prefix[o][i])
            out = intra[:, at] + (nn(query, high) + nn(query, low))
            inverse = lax.rsqrt(jnp.mean(out * out, axis=-1, keepdims=True) + EPS)
            normed = out * inverse
            rounded = normed.astype(BF16)
            attended[:, at] = rounded
            flipped[at, :] = rounded.astype(F32).T
            number = index[o] * heads + i
            first = number < low_grad.shape[1] // P_SIZE
            near = pl.ds(pl.multiple_of(number % (low_grad.shape[1] // P_SIZE) * P_SIZE, P_SIZE), P_SIZE)
            cot = jnp.where(first, low_grad[:, near], high_grad[:, near])
            mean = jnp.mean(cot * normed, axis=-1, keepdims=True)
            d = (inverse * (cot - normed * mean)).astype(BF16)
            d_out[:, at] = d
            d_prefix[order[o]][i] = tn(query, d)
            return carry

        lax.fori_loop(0, heads, one, 0)


def query_kernel(parts, index, k, v, d_out, *refs):
    prefix, (query_grad,) = refs[:parts], refs[parts:]
    heads = prefix[0].shape[0]
    lower = lower_of(k.shape[0])
    for o in range(parts):

        def one(i, carry, o=o):
            at = head_at(index[o], heads, i)
            d = d_out[:, at]
            high, low = halves(prefix[o][i])
            d_probs = jnp.where(lower, nt(d, v[:, at]), 0.0).astype(BF16)
            total = nn(d_probs, k[:, at]) + (nt(d, high) + nt(d, low))
            query_grad[:, at] = total.astype(BF16)
            return carry

        lax.fori_loop(0, heads, one, 0)


def key_value_kernel(parts, index, q, k, v, d_out, probs, *refs):
    suffix, (key_grad, value_grad) = refs[:parts], refs[parts:]
    heads = suffix[0].shape[0]
    lower = lower_of(k.shape[0])
    for o in range(parts):

        def one(i, carry, o=o):
            at = head_at(index[o], heads, i)
            d, value, key = d_out[:, at], v[:, at], k[:, at]
            high, low = halves(suffix[o][i])
            d_probs = jnp.where(lower, nt(d, value), 0.0).astype(BF16)
            d_key = tn(d_probs, q[:, at]) + (nt(value, high) + nt(value, low))
            key_grad[:, at] = d_key.astype(BF16)
            d_value = tn(probs[index[o] * heads + i], d) + (nn(key, high) + nn(key, low))
            value_grad[:, at] = d_value.astype(BF16)
            return carry

        lax.fori_loop(0, heads, one, 0)


def call(kernel, name, outs, flops, *args):
    moved = sum(a.size * a.dtype.itemsize for a in list(args) + list(outs))
    return pl.pallas_call(
        kernel,
        name=name,
        out_shape=tuple(outs),
        in_specs=[SMEM] + [VMEM] * (len(args) - 1),
        out_specs=(VMEM,) * len(outs),
        cost_estimate=pl.CostEstimate(flops=flops, bytes_accessed=moved, transcendentals=0),
        compiler_params=pltpu.CompilerParams(vmem_limit_bytes=40 << 20),
    )(*args)


def narrow_kernel(axis, *refs):
    out, at = refs[-1], 0
    for ref in refs[:-1]:
        size = ref.shape[axis]
        span = (pl.ds(at, size), slice(None)) if axis == 0 else (slice(None), pl.ds(at, size))
        out[span] = ref[...].astype(BF16)
        at += size


def narrow(pieces, axis):
    shape = list(pieces[0].shape)
    shape[axis] = sum(piece.shape[axis] for piece in pieces)
    moved = sum(6 * piece.size for piece in pieces)
    return pl.pallas_call(
        functools.partial(narrow_kernel, axis),
        name="narrow",
        out_shape=jax.ShapeDtypeStruct(tuple(shape), BF16),
        in_specs=[VMEM] * len(pieces),
        out_specs=VMEM,
        cost_estimate=pl.CostEstimate(flops=0, bytes_accessed=moved, transcendentals=0),
    )(*pieces)


def body(cores, count, queries, keys, values, out_grad, out_weight):
    dz, dy, dx = grid_of(count)
    plane = dy * dx
    tokens, width = queries.shape[1:]
    columns = out_grad.shape[-1]
    total_heads = width // P_SIZE
    heads = total_heads // plane
    block = width // (cores * count)
    q, k, v, cot = queries[0], keys[0], values[0], out_grad[0]

    core = lax.axis_index("dp")
    place = lax.axis_index("seq")
    x, y, z = place % dx, place // dx % dy, place // plane
    here = y * dx + x

    def send(value, to):
        pairs = []
        for d, a, b, c in itertools.product(range(cores), range(dz), range(dy), range(dx)):
            t = to(d, a, b, c)
            if t is not None:
                pairs.append((d * count + (a * dy + b) * dx + c, t[0] * count + (t[1] * dy + t[2]) * dx + t[3]))
        return lax.ppermute(value, AXES, pairs)

    def by(d=0, b=0, c=0):
        return lambda i, j, l, n: ((i + d) % cores, j, (l + b) % dy, (n + c) % dx)

    def along(step):
        return lambda i, j, l, n: (i, j + step, l, n) if 0 <= j + step < dz else None

    offsets = [(b, c) for b in range(dy) for c in range(dx)]
    target = [(y + b) % dy * dx + (x + c) % dx for b, c in offsets]
    source = [(y - b) % dy * dx + (x - c) % dx for b, c in offsets]
    order = [(-b % dy) * dx + (-c % dx) for b, c in offsets]
    target_index = jnp.stack(target).astype(jnp.int32)
    source_index = jnp.stack(source).astype(jnp.int32)

    part_shape = jax.ShapeDtypeStruct((heads, P_SIZE, P_SIZE), F32)
    wide = lambda kind: jax.ShapeDtypeStruct((tokens, width), kind)
    unit = 2 * tokens * width * P_SIZE

    def gather_plane(parts):
        return [parts[0]] + [send(parts[o], by(0, *offsets[o])) for o in range(1, plane)]

    def carry(received, sign, covers=()):
        total = functools.reduce(jnp.add, received)
        carried, running, step = jnp.zeros_like(total), total, 1
        covers = list(covers)
        while step < dz:
            arrived = send(running, along(sign * step))
            if covers:
                arrived, _ = lax.optimization_barrier((arrived, covers.pop(0)))
            carried, running, step = carried + arrived, running + arrived, 2 * step
        outs = []
        for o in range(plane):
            value = carried
            for s in range(plane):
                ahead = source[s] < target[o] if sign > 0 else source[s] > target[o]
                value = value + jnp.where(ahead, received[s], 0.0)
            outs.append(value)
        return total, outs

    states = call(functools.partial(state_kernel, plane), "states", [part_shape] * plane, unit, target_index, k, v)
    received = gather_plane(states)

    head_block = pl.BlockSpec((tokens, P_SIZE), lambda h: (0, h))
    probs, intra = pl.pallas_call(
        intra_kernel,
        name="intra",
        grid=(total_heads,),
        out_shape=(jax.ShapeDtypeStruct((total_heads, tokens, tokens), BF16), wide(F32)),
        in_specs=[head_block] * 3,
        out_specs=(pl.BlockSpec((1, tokens, tokens), lambda h: (h, 0, 0)), head_block),
        cost_estimate=pl.CostEstimate(flops=4 * unit, bytes_accessed=14 * tokens * width, transcendentals=0),
    )(q, k, v)
    middle = width // 2
    grads = [nt(cot, out_weight[:middle]), nt(cot, out_weight[middle:])]

    early = columns // EARLY
    half = (columns - early) // 2
    size = half // CHUNKS
    wide_cot = cot.astype(F32)
    pieces = [[wide_cot[:, g * half + n * size : g * half + (n + 1) * size] for n in range(CHUNKS)] for g in (0, 1)]
    reach = (dx, dy)
    shift = (lambda d, o: by(d, 0, o), lambda d, o: by(d, o, 0))

    def spread(group, n):
        own = pieces[group][n]
        near = [own] + [send(own, shift[group](0, o)) for o in range(1, reach[group])]
        rows = list(near)
        for d in range(1, cores):
            rows += [send(value, by(d)) for value in near]
        return rows

    received, wide_cot, _ = lax.optimization_barrier((received, wide_cot, intra))
    prefix_total, prefix_out = carry(received, 1, grads)
    pieces[0][0], pieces[1][0], _ = lax.optimization_barrier((pieces[0][0], pieces[1][0], prefix_total))
    prefix = gather_plane(prefix_out)
    for n in range(1, CHUNKS):
        pieces[0][n], pieces[1][n], _ = lax.optimization_barrier((pieces[0][n], pieces[1][n], prefix[-1]))
    spreads = [[spread(group, n) for n in range(CHUNKS)] for group in (0, 1)]
    pair_cot = wide_cot[:, 2 * half :]
    pair_cot = narrow([pair_cot] + [send(pair_cot, by(d)) for d in range(1, cores)], 0)

    done = call(
        functools.partial(output_kernel, plane, order),
        "outputs",
        [wide(BF16), jax.ShapeDtypeStruct((width, tokens), F32), wide(BF16)] + [part_shape] * plane,
        4 * unit,
        source_index, q, intra, *grads, *prefix,
    )
    attended, flipped, d_out, d_prefix = done[0], done[1], done[2], done[3:]

    d_received = gather_plane(d_prefix)

    folded = flipped.reshape(cores, dz, dy, dx, block, tokens)
    paired = [lax.dynamic_index_in_dim(folded, core, 0, False)]
    for d in range(1, cores):
        paired.append(send(lax.dynamic_index_in_dim(folded, (core + d) % cores, 0, False), by(d)))

    def features(group):
        mine, axis = ((x, 2), (y, 1))[group]
        near = reach[group]
        sides = []
        for d in range(cores):
            for o in range(near):
                if o == 0:
                    sides.append(lax.dynamic_index_in_dim(paired[d], mine, axis, False))
                    continue
                pick = lax.dynamic_index_in_dim(folded, (core + d) % cores, 0, False)
                pick = lax.dynamic_index_in_dim(pick, (mine + o) % near, axis, False)
                sides.append(send(pick, shift[group](d, o)))
        return [side.reshape(-1, tokens) for side in sides]

    sides = [features(0), features(1)]

    def line(sums):
        up = down = None
        for d in range(dz - 1, 0, -1):
            above = lax.dynamic_index_in_dim(sums, (z + d) % dz, 0, False)
            below = lax.dynamic_index_in_dim(sums, (z - d) % dz, 0, False)
            above = above if up is None else above + up
            below = below if down is None else below + down
            up = send(above, lambda i, j, l, n: (i, j + 1, l, n) if j + d < dz else None)
            down = send(below, lambda i, j, l, n: (i, j - 1, l, n) if j - d >= 0 else None)
        own = lax.dynamic_index_in_dim(sums, z, 0, False)
        return own if up is None else own + up + down

    pair_left = narrow([side.reshape(-1, tokens) for side in paired], 1)
    pair_sums = nn(pair_left, pair_cot).reshape(dz, plane * block, early)
    pair_line = line(pair_sums).reshape(plane, block, early)
    last = lax.dynamic_index_in_dim(pair_line, here, 0, False)
    for o in range(1, plane):
        last = last + send(lax.dynamic_index_in_dim(pair_line, target[o], 0, False), by(0, *offsets[o]))

    d_total, suffix_out = carry(d_received, -1)
    suffix = gather_plane(suffix_out)

    (query_grad,) = call(
        functools.partial(query_kernel, plane), "query", [wide(BF16)], 6 * unit, source_index, k, v, d_out, *prefix
    )
    rights = [[None] * CHUNKS for _ in (0, 1)]
    for group in (0, 1):
        rights[group][0] = narrow(spreads[group][0], 0)
    sides, _ = lax.optimization_barrier((sides, (rights[0][0], rights[1][0], d_total, pair_sums)))
    left = [narrow(side, 1) for side in sides]
    for group in (0, 1):
        for n in range(1, CHUNKS):
            rights[group][n] = narrow(spreads[group][n], 0)

    def first_stage(group, n):
        near = (dy, dx)[group]
        mine = (y, x)[group]
        other = (lambda o: by(0, o, 0), lambda o: by(0, 0, o))[group]
        right = rights[group][n]

        def partial(o):
            rows = lax.dynamic_index_in_dim(left[group].reshape(dz, near, block, -1), (mine + o) % near, 1, False)
            return nn(rows.reshape(dz * block, -1), right).reshape(dz, block, size)

        arrived = [send(partial(o), other(o)) for o in range(1, near)]
        return functools.reduce(jnp.add, [partial(0)] + arrived)

    key_grad, value_grad = call(
        functools.partial(key_value_kernel, plane),
        "keys",
        [wide(BF16), wide(BF16)],
        10 * unit,
        source_index, q, k, v, d_out, probs, *suffix,
    )

    chunks = []
    for n in range(CHUNKS):
        sums = jnp.concatenate([first_stage(0, n), first_stage(1, n)], axis=-1)
        if n == CHUNKS - 1:
            sums, _ = lax.optimization_barrier((sums, (key_grad, query_grad)))
        chunks.append(line(sums))
    weight_grad = jnp.concatenate([c[:, :size] for c in chunks] + [c[:, size:] for c in chunks] + [last], axis=-1)

    return attended[None], query_grad[None], key_grad[None], value_grad[None], weight_grad


def solution(mesh):
    spec = P("dp", "seq", None)
    return jax.shard_map(
        functools.partial(body, mesh.shape["dp"], mesh.shape["seq"]),
        mesh=mesh,
        in_specs=(spec,) * 4 + (P(),),
        out_specs=(spec,) * 4 + (P(AXES, None),),
        check_vma=False,
    )
```

```python
import functools
import itertools

import jax
import jax.numpy as jnp
from jax import lax
from jax.experimental import pallas as pl
from jax.experimental.pallas import tpu as pltpu
from jax.sharding import PartitionSpec as P

P_SIZE = 128
EPS = 1e-06
AXES = ("dp", "seq")
CHUNKS = 2
EARLY = 8
F32 = jnp.float32
BF16 = jnp.bfloat16


def grid_of(count):
    power = count.bit_length() - 1
    if 1 << power != count:
        return count, 1, 1
    z = -(-power // 3)
    y = -(-(power - z) // 2)
    return 1 << z, 1 << y, 1 << (power - z - y)


def tn(a, b):
    return lax.dot_general(a, b, (((0,), (0,)), ((), ())), preferred_element_type=F32)


def nt(a, b):
    return lax.dot_general(a, b, (((1,), (1,)), ((), ())), preferred_element_type=F32)


def nn(a, b):
    return lax.dot_general(a, b, (((1,), (0,)), ((), ())), preferred_element_type=F32)


def halves(x):
    high = x.astype(BF16)
    return high, (x - high.astype(F32)).astype(BF16)


def lower_of(count):
    rows = lax.broadcasted_iota(jnp.int32, (count, count), 0)
    return rows >= lax.broadcasted_iota(jnp.int32, (count, count), 1)


def columns_of(i):
    return pl.ds(pl.multiple_of(i * P_SIZE, P_SIZE), P_SIZE)


def each_part(parts, heads, one):
    for o in range(parts):

        @pl.when(pl.program_id(0) == o)
        def _(o=o):
            lax.fori_loop(0, heads, lambda i, carry: one(o, i) or carry, 0)


def state_kernel(parts, index, k, v, *outs):
    def one(o, i):
        outs[o][i] = tn(k[:, columns_of(i)], v[:, columns_of(i)])

    each_part(parts, outs[0].shape[0], one)


def intra_kernel(q, k, v, probs, intra):
    scores = nt(q[...], k[...])
    kept = jnp.where(lower_of(scores.shape[0]), scores, 0.0).astype(BF16)
    probs[0] = kept
    intra[...] = nn(kept, v[...])


def output_kernel(parts, order, cores, index, q, intra, low_grad, high_grad, *refs):
    prefix, (attended, d_out), refs = refs[:parts], refs[parts : parts + 2], refs[parts + 2 :]
    flipped, d_prefix = refs[:cores], refs[cores:]
    heads = prefix[0].shape[0]
    span = flipped[0].shape[0]
    part = index[pl.program_id(0)]

    def one(o, i):
        at = columns_of(i)
        query = q[:, at]
        high, low = halves(prefix[o][i])
        out = intra[:, at] + (nn(query, high) + nn(query, low))
        inverse = lax.rsqrt(jnp.mean(out * out, axis=-1, keepdims=True) + EPS)
        normed = out * inverse
        rounded = normed.astype(BF16)
        attended[:, at] = rounded
        row = (part * heads + i) * P_SIZE
        across = rounded.astype(F32).T
        owner = lax.rem(row // span + cores - index[parts], cores)
        for d in range(cores):

            @pl.when(owner == d)
            def _(d=d):
                flipped[d][pl.ds(pl.multiple_of(lax.rem(row, span), P_SIZE), P_SIZE), :] = across

        cot = jnp.where(part < parts // 2, low_grad[:, at], high_grad[:, at])
        mean = jnp.mean(cot * normed, axis=-1, keepdims=True)
        d = (inverse * (cot - normed * mean)).astype(BF16)
        d_out[:, at] = d
        d_prefix[order[o]][i] = tn(query, d)

    each_part(parts, heads, one)


def query_kernel(parts, index, k, v, d_out, *refs):
    prefix, (query_grad,) = refs[:parts], refs[parts:]
    lower = lower_of(k.shape[0])

    def one(o, i):
        at = columns_of(i)
        d = d_out[:, at]
        high, low = halves(prefix[o][i])
        d_probs = jnp.where(lower, nt(d, v[:, at]), 0.0).astype(BF16)
        total = nn(d_probs, k[:, at]) + (nt(d, high) + nt(d, low))
        query_grad[:, at] = total.astype(BF16)

    each_part(parts, prefix[0].shape[0], one)


def key_value_kernel(parts, index, q, k, v, d_out, probs, *refs):
    suffix, (key_grad, value_grad) = refs[:parts], refs[parts:]
    lower = lower_of(k.shape[0])

    def one(o, i):
        at = columns_of(i)
        d, value, key = d_out[:, at], v[:, at], k[:, at]
        high, low = halves(suffix[o][i])
        d_probs = jnp.where(lower, nt(d, value), 0.0).astype(BF16)
        d_key = tn(d_probs, q[:, at]) + (nt(value, high) + nt(value, low))
        key_grad[:, at] = d_key.astype(BF16)
        d_value = tn(probs[i], d) + (nn(key, high) + nn(key, low))
        value_grad[:, at] = d_value.astype(BF16)

    each_part(parts, suffix[0].shape[0], one)


def product_kernel(count, index, *refs):
    lefts, rights, outs, (rows, right) = refs[:count], refs[count : 2 * count], refs[2 * count : -2], refs[-2:]
    outer, near, inner, tokens = lefts[0].shape
    for s in range(count):
        right[s * tokens : (s + 1) * tokens, :] = rights[s][...].astype(BF16)
    for o in range(near):
        pick = lax.rem(index[0] + o, near)
        for s in range(count):
            for n in range(outer):
                rows[n * inner : (n + 1) * inner, s * tokens : (s + 1) * tokens] = lefts[s][n, pick].astype(BF16)
        outs[o][...] = nn(rows[...], right[...])


def product(name, index, lefts, rights, place, size):
    outer, near, inner, tokens = lefts[0].shape
    total = tokens * len(lefts)
    whole = pl.BlockSpec((outer, near, inner, tokens), lambda i, table: (0, 0, 0, 0))
    specs = []
    for right in rights:
        block = place if right.shape[1] > size else 0
        specs.append(pl.BlockSpec((tokens, size), lambda i, table, block=block: (0, block)))
    flops = 2 * near * outer * inner * total * size
    outs = pl.pallas_call(
        functools.partial(product_kernel, len(lefts)),
        name=name,
        grid_spec=pltpu.PrefetchScalarGridSpec(
            num_scalar_prefetch=1,
            grid=(1,),
            in_specs=[whole] * len(lefts) + specs,
            out_specs=[pl.BlockSpec((outer * inner, size), lambda i, table: (0, 0))] * near,
            scratch_shapes=[pltpu.VMEM((outer * inner, total), BF16), pltpu.VMEM((total, size), BF16)],
        ),
        out_shape=[jax.ShapeDtypeStruct((outer * inner, size), F32)] * near,
        cost_estimate=pl.CostEstimate(
            flops=flops, bytes_accessed=4 * (total * size + near * outer * inner * (total + size)), transcendentals=0
        ),
        compiler_params=pltpu.CompilerParams(vmem_limit_bytes=48 << 20),
    )(index.reshape(1).astype(jnp.int32), *lefts, *rights)
    return [out.reshape(outer, inner, size) for out in outs]


def by_parts(kernel, name, parts, flops, index, inputs, outputs):
    def spec(value, kind):
        tall = value.shape[0]
        if kind == "part":
            return pl.BlockSpec((tall, value.shape[1] // parts), lambda i, table: (0, table[i]))
        if kind == "low":
            return pl.BlockSpec((tall, 2 * value.shape[1] // parts), lambda i, table: (0, jnp.minimum(table[i], parts // 2 - 1)))
        if kind == "high":
            return pl.BlockSpec((tall, 2 * value.shape[1] // parts), lambda i, table: (0, jnp.maximum(table[i] - parts // 2, 0)))
        if kind == "heads":
            return pl.BlockSpec((tall // parts,) + value.shape[1:], lambda i, table: (table[i], 0, 0))
        return pl.BlockSpec(value.shape, lambda i, table: (0,) * len(value.shape))

    moved = sum(a.size * a.dtype.itemsize for a, _ in list(inputs) + list(outputs))
    return pl.pallas_call(
        kernel,
        name=name,
        grid_spec=pltpu.PrefetchScalarGridSpec(
            num_scalar_prefetch=1,
            grid=(parts,),
            in_specs=[spec(*pair) for pair in inputs],
            out_specs=[spec(*pair) for pair in outputs],
        ),
        out_shape=[shape for shape, _ in outputs],
        cost_estimate=pl.CostEstimate(flops=flops, bytes_accessed=moved, transcendentals=0),
        compiler_params=pltpu.CompilerParams(vmem_limit_bytes=48 << 20),
    )(index, *[value for value, _ in inputs])


def body(cores, count, queries, keys, values, out_grad, out_weight):
    dz, dy, dx = grid_of(count)
    plane = dy * dx
    tokens, width = queries.shape[1:]
    columns = out_grad.shape[-1]
    total_heads = width // P_SIZE
    heads = total_heads // plane
    block = width // (cores * count)
    q, k, v, cot = queries[0], keys[0], values[0], out_grad[0]

    core = lax.axis_index("dp")
    place = lax.axis_index("seq")
    x, y, z = place % dx, place // dx % dy, place // plane
    here = y * dx + x

    def send(value, to):
        pairs = []
        for d, a, b, c in itertools.product(range(cores), range(dz), range(dy), range(dx)):
            t = to(d, a, b, c)
            if t is not None:
                pairs.append((d * count + (a * dy + b) * dx + c, t[0] * count + (t[1] * dy + t[2]) * dx + t[3]))
        return lax.ppermute(value, AXES, pairs)

    def by(d=0, b=0, c=0):
        return lambda i, j, l, n: ((i + d) % cores, j, (l + b) % dy, (n + c) % dx)

    def along(step):
        return lambda i, j, l, n: (i, j + step, l, n) if 0 <= j + step < dz else None

    offsets = [(b, c) for b in range(dy) for c in range(dx)]
    target = [(y + b) % dy * dx + (x + c) % dx for b, c in offsets]
    source = [(y - b) % dy * dx + (x - c) % dx for b, c in offsets]
    order = [(-b % dy) * dx + (-c % dx) for b, c in offsets]
    target_index = jnp.stack(target).astype(jnp.int32)
    source_index = jnp.stack(source + [core]).astype(jnp.int32)

    part_shape = jax.ShapeDtypeStruct((heads, P_SIZE, P_SIZE), F32)
    wide = lambda kind: jax.ShapeDtypeStruct((tokens, width), kind)
    unit = 2 * tokens * width * P_SIZE

    def gather_plane(parts):
        return [parts[0]] + [send(parts[o], by(0, *offsets[o])) for o in range(1, plane)]

    def carry(received, sign, covers=()):
        total = functools.reduce(jnp.add, received)
        carried, running, step = jnp.zeros_like(total), total, 1
        covers = list(covers)
        while step < dz:
            arrived = send(running, along(sign * step))
            if covers:
                arrived, _ = lax.optimization_barrier((arrived, covers.pop(0)))
            carried, running, step = carried + arrived, running + arrived, 2 * step
        outs = []
        for o in range(plane):
            value = carried
            for s in range(plane):
                ahead = source[s] < target[o] if sign > 0 else source[s] > target[o]
                value = value + jnp.where(ahead, received[s], 0.0)
            outs.append(value)
        return total, outs

    states = by_parts(
        functools.partial(state_kernel, plane), "states", plane, unit, target_index,
        [(k, "part"), (v, "part")], [(part_shape, "all")] * plane,
    )
    with jax.named_scope("to_plane"):
        received = gather_plane(states)

    head_block = pl.BlockSpec((tokens, P_SIZE), lambda h: (0, h))
    probs, intra = pl.pallas_call(
        intra_kernel,
        name="intra",
        grid=(total_heads,),
        out_shape=(jax.ShapeDtypeStruct((total_heads, tokens, tokens), BF16), wide(F32)),
        in_specs=[head_block] * 3,
        out_specs=(pl.BlockSpec((1, tokens, tokens), lambda h: (h, 0, 0)), head_block),
        cost_estimate=pl.CostEstimate(flops=4 * unit, bytes_accessed=14 * tokens * width, transcendentals=0),
    )(q, k, v)
    middle = width // 2
    with jax.named_scope("low_grad"):
        low_grad = nt(cot, out_weight[:middle])
    with jax.named_scope("high_grad"):
        high_grad = nt(cot, out_weight[middle:])

    early = columns // EARLY
    half = (columns - early) // 2
    size = half // CHUNKS
    reach = (dx, dy)
    shift = (lambda d, o: by(d, 0, o), lambda d, o: by(d, o, 0))
    with jax.named_scope("cot_pair"):
        wide_cot = cot.astype(F32)
        paired_cot = [cot] + [send(wide_cot, by(d)) for d in range(1, cores)]

    def cut(group, n):
        at = (group * CHUNKS + n) * size
        return cot[:, at : at + size].astype(F32)

    def spread(group, n, piece):
        with jax.named_scope(f"cot_{group}_{n}"):
            near = [send(piece, shift[group](0, o)) for o in range(1, reach[group])]
        rows = [paired_cot[0]] + near
        with jax.named_scope(f"pass_{group}_{n}"):
            for d in range(1, cores):
                rows += [paired_cot[d]] + [send(value, by(d)) for value in near]
        return rows

    cuts = [[cut(group, n) for n in range(CHUNKS)] for group in (0, 1)]
    received, cuts, _ = lax.optimization_barrier((received, cuts, intra))
    with jax.named_scope("prefix"):
        prefix_total, prefix_out = carry(received, 1, (low_grad, high_grad))
    cuts[0][0], cuts[1][0], _ = lax.optimization_barrier((cuts[0][0], cuts[1][0], prefix_total))
    with jax.named_scope("from_plane"):
        prefix = gather_plane(prefix_out)
    for n in range(1, CHUNKS):
        cuts[0][n], cuts[1][n], _ = lax.optimization_barrier((cuts[0][n], cuts[1][n], prefix[-1]))
    rights = [[spread(group, n, cuts[group][n]) for n in range(CHUNKS)] for group in (0, 1)]

    flat = jax.ShapeDtypeStruct((width // cores, tokens), F32)
    done = by_parts(
        functools.partial(output_kernel, plane, order, cores), "outputs", plane, 4 * unit, source_index,
        [(q, "part"), (intra, "part"), (low_grad, "low"), (high_grad, "high")] + [(p, "all") for p in prefix],
        [(wide(BF16), "part"), (wide(BF16), "part")] + [(flat, "all")] * cores + [(part_shape, "all")] * plane,
    )
    attended, d_out, flipped, d_prefix = done[0], done[1], done[2 : 2 + cores], done[2 + cores :]

    with jax.named_scope("feature_pair"):
        paired = [flipped[0]] + [send(flipped[d], by(d)) for d in range(1, cores)]
    with jax.named_scope("d_to_plane"):
        d_received = gather_plane(d_prefix)

    def features(group):
        shape = ((dz * dy, dx, block, tokens), (dz, dy, dx * block, tokens))[group]
        mine, near = ((x, dx), (y, dy))[group]
        sides = []
        for d in range(cores):
            sides.append(lax.dynamic_index_in_dim(paired[d].reshape(shape), mine, 1, False))
            with jax.named_scope(f"feature_{group}"):
                for o in range(1, near):
                    pick = lax.dynamic_index_in_dim(flipped[d].reshape(shape), (mine + o) % near, 1, False)
                    sides.append(send(pick, shift[group](d, o)))
        inner = ((dz, dy, block, tokens), (dz, dx, block, tokens))[group]
        return [side.reshape(inner) for side in sides]

    lefts = [features(0), features(1)]

    def halve(outs, bit):
        total = outs[0] + send(outs[1], lambda i, j, l, n: (i, j ^ (1 << bit), l, n))
        if 2 << bit == dz:
            return total[0]
        blocks = total.reshape((-1, 2) + total.shape[1:])
        mine = (z >> (bit + 1)) & 1
        return halve([lax.dynamic_index_in_dim(blocks, (mine + o) % 2, 1, False) for o in (0, 1)], bit + 1)

    def reduce_over(value, mine, near, to):
        total = lax.dynamic_index_in_dim(value, mine, 0, False)
        for o in range(1, near):
            total = total + send(lax.dynamic_index_in_dim(value, (mine + o) % near, 0, False), to(o))
        return total

    low_bit = 2 if dz > 1 else 1
    pair_view = [side.reshape(dz // low_bit, low_bit, plane * block, tokens) for side in paired]
    with jax.named_scope("early"):
        outs = product("early", z % low_bit, pair_view, paired_cot, 2 * half // early, early)
        last = halve(outs, 0) if dz > 1 else outs[0][0]
        last = reduce_over(last.reshape(dy, dx * block, early), y, dy, lambda o: by(0, o, 0))
        last = reduce_over(last.reshape(dx, block, early), x, dx, lambda o: by(0, 0, o))

    with jax.named_scope("suffix"):
        d_total, suffix_out = carry(d_received, -1)
    with jax.named_scope("d_from_plane"):
        suffix = gather_plane(suffix_out)

    (query_grad,) = by_parts(
        functools.partial(query_kernel, plane), "query", plane, 6 * unit, source_index,
        [(k, "part"), (v, "part"), (d_out, "part")] + [(p, "all") for p in prefix], [(wide(BF16), "part")],
    )
    key_grad, value_grad = by_parts(
        functools.partial(key_value_kernel, plane), "keys", plane, 10 * unit, source_index,
        [(q, "part"), (k, "part"), (v, "part"), (d_out, "part"), (probs, "heads")] + [(p, "all") for p in suffix],
        [(wide(BF16), "part"), (wide(BF16), "part")],
    )

    def first_stage(group, n):
        mine = (y, x)[group]
        other = (lambda o: by(0, o, 0), lambda o: by(0, 0, o))[group]
        with jax.named_scope(f"stage_{group}_{n}"):
            outs = product(f"product_{group}_{n}", mine, lefts[group], rights[group][n], group * CHUNKS + n, size)
            return functools.reduce(jnp.add, outs[:1] + [send(out, other(o)) for o, out in enumerate(outs) if o])

    chunks = []
    for n in range(CHUNKS):
        sums = jnp.concatenate([first_stage(0, n), first_stage(1, n)], axis=-1)
        with jax.named_scope(f"line_{n}"):
            if dz > 1:
                blocks = sums.reshape((dz // 2, 2) + sums.shape[1:])
                outs = [lax.dynamic_index_in_dim(blocks, (z + o) % 2, 1, False) for o in (0, 1)]
                chunks.append(halve(outs, 0))
            else:
                chunks.append(sums[0])
    weight_grad = jnp.concatenate([c[:, :size] for c in chunks] + [c[:, size:] for c in chunks] + [last], axis=-1)
    return attended[None], query_grad[None], key_grad[None], value_grad[None], weight_grad


def solution(mesh):
    spec = P("dp", "seq", None)
    return jax.shard_map(
        functools.partial(body, mesh.shape["dp"], mesh.shape["seq"]),
        mesh=mesh,
        in_specs=(spec,) * 4 + (P(),),
        out_specs=(spec,) * 4 + (P(AXES, None),),
        check_vma=False,
    )
```

```python
import functools
import itertools

import jax
import jax.numpy as jnp
from jax import lax
from jax.experimental import pallas as pl
from jax.experimental.pallas import tpu as pltpu
from jax.sharding import PartitionSpec as P

P_SIZE = 128
EPS = 1e-06
AXES = ("dp", "seq")
CHUNKS = 2
EARLY = 8
F32 = jnp.float32
BF16 = jnp.bfloat16


def grid_of(count):
    power = count.bit_length() - 1
    if 1 << power != count:
        return count, 1, 1
    z = -(-power // 3)
    y = -(-(power - z) // 2)
    return 1 << z, 1 << y, 1 << (power - z - y)


def tn(a, b):
    return lax.dot_general(a, b, (((0,), (0,)), ((), ())), preferred_element_type=F32)


def nt(a, b):
    return lax.dot_general(a, b, (((1,), (1,)), ((), ())), preferred_element_type=F32)


def nn(a, b):
    return lax.dot_general(a, b, (((1,), (0,)), ((), ())), preferred_element_type=F32)


def halves(x):
    high = x.astype(BF16)
    return high, (x - high.astype(F32)).astype(BF16)


def lower_of(count):
    rows = lax.broadcasted_iota(jnp.int32, (count, count), 0)
    return rows >= lax.broadcasted_iota(jnp.int32, (count, count), 1)


def columns_of(i):
    return pl.ds(pl.multiple_of(i * P_SIZE, P_SIZE), P_SIZE)


def each_part(parts, heads, one):
    for o in range(parts):

        @pl.when(pl.program_id(0) == o)
        def _(o=o):
            lax.fori_loop(0, heads, lambda i, carry: one(o, i) or carry, 0)


def state_kernel(parts, index, k, v, *outs):
    def one(o, i):
        outs[o][i] = tn(k[:, columns_of(i)], v[:, columns_of(i)])

    each_part(parts, outs[0].shape[0], one)


def intra_kernel(q, k, v, probs, intra):
    scores = nt(q[...], k[...])
    kept = jnp.where(lower_of(scores.shape[0]), scores, 0.0).astype(BF16)
    probs[0] = kept
    intra[...] = nn(kept, v[...])


def output_kernel(parts, order, cores, index, q, intra, low_grad, high_grad, *refs):
    prefix, (attended, d_out), refs = refs[:parts], refs[parts : parts + 2], refs[parts + 2 :]
    flipped, d_prefix = refs[:cores], refs[cores:]
    heads = prefix[0].shape[0]
    span = flipped[0].shape[0]
    part = index[pl.program_id(0)]

    def one(o, i):
        at = columns_of(i)
        query = q[:, at]
        high, low = halves(prefix[o][i])
        out = intra[:, at] + (nn(query, high) + nn(query, low))
        inverse = lax.rsqrt(jnp.mean(out * out, axis=-1, keepdims=True) + EPS)
        normed = out * inverse
        rounded = normed.astype(BF16)
        attended[:, at] = rounded
        row = (part * heads + i) * P_SIZE
        across = rounded.astype(F32).T
        owner = lax.rem(row // span + cores - index[parts], cores)
        for d in range(cores):

            @pl.when(owner == d)
            def _(d=d):
                flipped[d][pl.ds(pl.multiple_of(lax.rem(row, span), P_SIZE), P_SIZE), :] = across

        cot = jnp.where(part < parts // 2, low_grad[:, at], high_grad[:, at])
        mean = jnp.mean(cot * normed, axis=-1, keepdims=True)
        d = (inverse * (cot - normed * mean)).astype(BF16)
        d_out[:, at] = d
        d_prefix[order[o]][i] = tn(query, d)

    each_part(parts, heads, one)


def query_kernel(parts, index, k, v, d_out, *refs):
    prefix, (query_grad,) = refs[:parts], refs[parts:]
    lower = lower_of(k.shape[0])

    def one(o, i):
        at = columns_of(i)
        d = d_out[:, at]
        high, low = halves(prefix[o][i])
        d_probs = jnp.where(lower, nt(d, v[:, at]), 0.0).astype(BF16)
        total = nn(d_probs, k[:, at]) + (nt(d, high) + nt(d, low))
        query_grad[:, at] = total.astype(BF16)

    each_part(parts, prefix[0].shape[0], one)


def key_value_kernel(parts, index, q, k, v, d_out, probs, *refs):
    suffix, (key_grad, value_grad) = refs[:parts], refs[parts:]
    lower = lower_of(k.shape[0])

    def one(o, i):
        at = columns_of(i)
        d, value, key = d_out[:, at], v[:, at], k[:, at]
        high, low = halves(suffix[o][i])
        d_probs = jnp.where(lower, nt(d, value), 0.0).astype(BF16)
        d_key = tn(d_probs, q[:, at]) + (nt(value, high) + nt(value, low))
        key_grad[:, at] = d_key.astype(BF16)
        d_value = tn(probs[i], d) + (nn(key, high) + nn(key, low))
        value_grad[:, at] = d_value.astype(BF16)

    each_part(parts, suffix[0].shape[0], one)


def product_kernel(count, index, *refs):
    lefts, rights, outs, (rows, right) = refs[:count], refs[count : 2 * count], refs[2 * count : -2], refs[-2:]
    outer, near, inner, tokens = lefts[0].shape
    for s in range(count):
        right[s * tokens : (s + 1) * tokens, :] = rights[s][...].astype(BF16)
    for o in range(near):
        pick = lax.rem(index[0] + o, near)
        for s in range(count):
            for n in range(outer):
                rows[n * inner : (n + 1) * inner, s * tokens : (s + 1) * tokens] = lefts[s][n, pick].astype(BF16)
        outs[o][...] = nn(rows[...], right[...])


def product(index, lefts, rights, place, size):
    outer, near, inner, tokens = lefts[0].shape
    total = tokens * len(lefts)
    whole = pl.BlockSpec((outer, near, inner, tokens), lambda i, table: (0, 0, 0, 0))
    specs = []
    for right in rights:
        block = place if right.shape[1] > size else 0
        specs.append(pl.BlockSpec((tokens, size), lambda i, table, block=block: (0, block)))
    flops = 2 * near * outer * inner * total * size
    outs = pl.pallas_call(
        functools.partial(product_kernel, len(lefts)),
        grid_spec=pltpu.PrefetchScalarGridSpec(
            num_scalar_prefetch=1,
            grid=(1,),
            in_specs=[whole] * len(lefts) + specs,
            out_specs=[pl.BlockSpec((outer * inner, size), lambda i, table: (0, 0))] * near,
            scratch_shapes=[pltpu.VMEM((outer * inner, total), BF16), pltpu.VMEM((total, size), BF16)],
        ),
        out_shape=[jax.ShapeDtypeStruct((outer * inner, size), F32)] * near,
        cost_estimate=pl.CostEstimate(
            flops=flops, bytes_accessed=4 * (total * size + near * outer * inner * (total + size)), transcendentals=0
        ),
        compiler_params=pltpu.CompilerParams(vmem_limit_bytes=48 << 20),
    )(index.reshape(1).astype(jnp.int32), *lefts, *rights)
    return [out.reshape(outer, inner, size) for out in outs]


def by_parts(kernel, parts, flops, index, inputs, outputs):
    def spec(value, kind):
        tall = value.shape[0]
        if kind == "part":
            return pl.BlockSpec((tall, value.shape[1] // parts), lambda i, table: (0, table[i]))
        if kind == "low":
            return pl.BlockSpec((tall, 2 * value.shape[1] // parts), lambda i, table: (0, jnp.minimum(table[i], parts // 2 - 1)))
        if kind == "high":
            return pl.BlockSpec((tall, 2 * value.shape[1] // parts), lambda i, table: (0, jnp.maximum(table[i] - parts // 2, 0)))
        if kind == "heads":
            return pl.BlockSpec((tall // parts,) + value.shape[1:], lambda i, table: (table[i], 0, 0))
        return pl.BlockSpec(value.shape, lambda i, table: (0,) * len(value.shape))

    moved = sum(a.size * a.dtype.itemsize for a, _ in list(inputs) + list(outputs))
    return pl.pallas_call(
        kernel,
        grid_spec=pltpu.PrefetchScalarGridSpec(
            num_scalar_prefetch=1,
            grid=(parts,),
            in_specs=[spec(*pair) for pair in inputs],
            out_specs=[spec(*pair) for pair in outputs],
        ),
        out_shape=[shape for shape, _ in outputs],
        cost_estimate=pl.CostEstimate(flops=flops, bytes_accessed=moved, transcendentals=0),
        compiler_params=pltpu.CompilerParams(vmem_limit_bytes=48 << 20),
    )(index, *[value for value, _ in inputs])


def body(cores, count, queries, keys, values, out_grad, out_weight):
    dz, dy, dx = grid_of(count)
    plane = dy * dx
    tokens, width = queries.shape[1:]
    columns = out_grad.shape[-1]
    total_heads = width // P_SIZE
    heads = total_heads // plane
    block = width // (cores * count)
    q, k, v, cot = queries[0], keys[0], values[0], out_grad[0]

    core = lax.axis_index("dp")
    place = lax.axis_index("seq")
    x, y, z = place % dx, place // dx % dy, place // plane

    def send(value, to):
        pairs = []
        for d, a, b, c in itertools.product(range(cores), range(dz), range(dy), range(dx)):
            t = to(d, a, b, c)
            if t is not None:
                pairs.append((d * count + (a * dy + b) * dx + c, t[0] * count + (t[1] * dy + t[2]) * dx + t[3]))
        return lax.ppermute(value, AXES, pairs)

    def by(d=0, b=0, c=0):
        return lambda i, j, l, n: ((i + d) % cores, j, (l + b) % dy, (n + c) % dx)

    def along(step):
        return lambda i, j, l, n: (i, j + step, l, n) if 0 <= j + step < dz else None

    offsets = [(b, c) for b in range(dy) for c in range(dx)]
    target = [(y + b) % dy * dx + (x + c) % dx for b, c in offsets]
    source = [(y - b) % dy * dx + (x - c) % dx for b, c in offsets]
    order = [(-b % dy) * dx + (-c % dx) for b, c in offsets]
    target_index = jnp.stack(target).astype(jnp.int32)
    source_index = jnp.stack(source + [core]).astype(jnp.int32)

    part_shape = jax.ShapeDtypeStruct((heads, P_SIZE, P_SIZE), F32)
    wide = lambda kind: jax.ShapeDtypeStruct((tokens, width), kind)
    unit = 2 * tokens * width * P_SIZE

    def gather_plane(parts):
        return [parts[0]] + [send(parts[o], by(0, *offsets[o])) for o in range(1, plane)]

    def carry(received, sign, covers=()):
        total = functools.reduce(jnp.add, received)
        carried, running, step = jnp.zeros_like(total), total, 1
        covers = list(covers)
        while step < dz:
            arrived = send(running, along(sign * step))
            if covers:
                arrived, _ = lax.optimization_barrier((arrived, covers.pop(0)))
            carried, running, step = carried + arrived, running + arrived, 2 * step
        outs = []
        for o in range(plane):
            value = carried
            for s in range(plane):
                ahead = source[s] < target[o] if sign > 0 else source[s] > target[o]
                value = value + jnp.where(ahead, received[s], 0.0)
            outs.append(value)
        return total, outs

    states = by_parts(
        functools.partial(state_kernel, plane), plane, unit, target_index,
        [(k, "part"), (v, "part")], [(part_shape, "all")] * plane,
    )
    received = gather_plane(states)

    head_block = pl.BlockSpec((tokens, P_SIZE), lambda h: (0, h))
    probs, intra = pl.pallas_call(
        intra_kernel,
        name="intra",
        grid=(total_heads,),
        out_shape=(jax.ShapeDtypeStruct((total_heads, tokens, tokens), BF16), wide(F32)),
        in_specs=[head_block] * 3,
        out_specs=(pl.BlockSpec((1, tokens, tokens), lambda h: (h, 0, 0)), head_block),
        cost_estimate=pl.CostEstimate(flops=4 * unit, bytes_accessed=14 * tokens * width, transcendentals=0),
    )(q, k, v)
    middle = width // 2
    low_grad = nt(cot, out_weight[:middle])
    high_grad = nt(cot, out_weight[middle:])

    early = columns // EARLY
    half = (columns - early) // 2
    size = half // CHUNKS
    reach = (dx, dy)
    shift = (lambda d, o: by(d, 0, o), lambda d, o: by(d, o, 0))
    wide_cot = cot.astype(F32)
    paired_cot = [cot] + [send(wide_cot, by(d)) for d in range(1, cores)]

    def cut(group, n):
        at = (group * CHUNKS + n) * size
        return cot[:, at : at + size].astype(F32)

    def spread(group, piece):
        near = [send(piece, shift[group](0, o)) for o in range(1, reach[group])]
        rows = [paired_cot[0]] + near
        for d in range(1, cores):
            rows += [paired_cot[d]] + [send(value, by(d)) for value in near]
        return rows

    cuts = [[cut(group, n) for n in range(CHUNKS)] for group in (0, 1)]
    received, cuts, _ = lax.optimization_barrier((received, cuts, intra))
    prefix_total, prefix_out = carry(received, 1, (low_grad, high_grad))
    cuts[0][0], cuts[1][0], _ = lax.optimization_barrier((cuts[0][0], cuts[1][0], prefix_total))
    prefix = gather_plane(prefix_out)
    for n in range(1, CHUNKS):
        cuts[0][n], cuts[1][n], _ = lax.optimization_barrier((cuts[0][n], cuts[1][n], prefix[-1]))
    rights = [[spread(group, cuts[group][n]) for n in range(CHUNKS)] for group in (0, 1)]

    flat = jax.ShapeDtypeStruct((width // cores, tokens), F32)
    done = by_parts(
        functools.partial(output_kernel, plane, order, cores), plane, 4 * unit, source_index,
        [(q, "part"), (intra, "part"), (low_grad, "low"), (high_grad, "high")] + [(p, "all") for p in prefix],
        [(wide(BF16), "part"), (wide(BF16), "part")] + [(flat, "all")] * cores + [(part_shape, "all")] * plane,
    )
    attended, d_out, flipped, d_prefix = done[0], done[1], done[2 : 2 + cores], done[2 + cores :]

    paired = [flipped[0]] + [send(flipped[d], by(d)) for d in range(1, cores)]
    d_received = gather_plane(d_prefix)

    def features(group):
        shape = ((dz * dy, dx, block, tokens), (dz, dy, dx * block, tokens))[group]
        mine, near = ((x, dx), (y, dy))[group]
        sides = []
        for d in range(cores):
            sides.append(lax.dynamic_index_in_dim(paired[d].reshape(shape), mine, 1, False))
            for o in range(1, near):
                pick = lax.dynamic_index_in_dim(flipped[d].reshape(shape), (mine + o) % near, 1, False)
                sides.append(send(pick, shift[group](d, o)))
        inner = ((dz, dy, block, tokens), (dz, dx, block, tokens))[group]
        return [side.reshape(inner) for side in sides]

    lefts = [features(0), features(1)]

    def halve(outs, bit):
        total = outs[0] + send(outs[1], lambda i, j, l, n: (i, j ^ (1 << bit), l, n))
        if 2 << bit == dz:
            return total[0]
        blocks = total.reshape((-1, 2) + total.shape[1:])
        mine = (z >> (bit + 1)) & 1
        return halve([lax.dynamic_index_in_dim(blocks, (mine + o) % 2, 1, False) for o in (0, 1)], bit + 1)

    def reduce_over(value, mine, near, to):
        total = lax.dynamic_index_in_dim(value, mine, 0, False)
        for o in range(1, near):
            total = total + send(lax.dynamic_index_in_dim(value, (mine + o) % near, 0, False), to(o))
        return total

    low_bit = 2 if dz > 1 else 1
    pair_view = [side.reshape(dz // low_bit, low_bit, plane * block, tokens) for side in paired]
    outs = product(z % low_bit, pair_view, paired_cot, 2 * half // early, early)
    last = halve(outs, 0) if dz > 1 else outs[0][0]
    last = reduce_over(last.reshape(dy, dx * block, early), y, dy, lambda o: by(0, o, 0))
    last = reduce_over(last.reshape(dx, block, early), x, dx, lambda o: by(0, 0, o))

    _, suffix_out = carry(d_received, -1)
    suffix = gather_plane(suffix_out)

    (query_grad,) = by_parts(
        functools.partial(query_kernel, plane), plane, 6 * unit, source_index,
        [(k, "part"), (v, "part"), (d_out, "part")] + [(p, "all") for p in prefix], [(wide(BF16), "part")],
    )

    def first_stage(group, n):
        mine = (y, x)[group]
        other = (lambda o: by(0, o, 0), lambda o: by(0, 0, o))[group]
        outs = product(mine, lefts[group], rights[group][n], group * CHUNKS + n, size)
        return functools.reduce(jnp.add, outs[:1] + [send(out, other(o)) for o, out in enumerate(outs) if o])

    sums = [jnp.concatenate([first_stage(0, n), first_stage(1, n)], axis=-1) for n in range(CHUNKS)]
    suffix, _ = lax.optimization_barrier((suffix, sums[-1]))
    key_grad, value_grad = by_parts(
        functools.partial(key_value_kernel, plane), plane, 10 * unit, source_index,
        [(q, "part"), (k, "part"), (v, "part"), (d_out, "part"), (probs, "heads")] + [(p, "all") for p in suffix],
        [(wide(BF16), "part"), (wide(BF16), "part")],
    )

    chunks = []
    for n in range(CHUNKS):
        if dz > 1:
            blocks = sums[n].reshape((dz // 2, 2) + sums[n].shape[1:])
            outs = [lax.dynamic_index_in_dim(blocks, (z + o) % 2, 1, False) for o in (0, 1)]
            chunks.append(halve(outs, 0))
        else:
            chunks.append(sums[n][0])
    weight_grad = jnp.concatenate([c[:, :size] for c in chunks] + [c[:, size:] for c in chunks] + [last], axis=-1)
    return attended[None], query_grad[None], key_grad[None], value_grad[None], weight_grad


def solution(mesh):
    spec = P("dp", "seq", None)
    return jax.shard_map(
        functools.partial(body, mesh.shape["dp"], mesh.shape["seq"]),
        mesh=mesh,
        in_specs=(spec,) * 4 + (P(),),
        out_specs=(spec,) * 4 + (P(AXES, None),),
        check_vma=False,
    )
```
